32 devices in a mesh: ctx: 8 (over z, core), head: 4 (over y, x).
Axes of the slice: x: 2, y: 2, z: 4, core: 2. Of those that a mesh axis runs over, the one named last changes fastest.
Arguments:
- query: bfloat16 [4096, 64, 128], P('ctx', 'head'), may hold values from -8 to 8
- keys: bfloat16 [4096, 8, 128], P('ctx', 'head'), may hold values from -8 to 8
- values: bfloat16 [4096, 8, 128], P('ctx', 'head'), may hold values from -6 to 6
- k_scale: bfloat16 [16, 8], P('ctx', 'head'), may hold values from 0.59765625 to 1.59375
- v_scale: bfloat16 [16, 8], P('ctx', 'head'), may hold values from 0.5 to 2
- block_place: int32 [16], P('ctx'), may hold values from 0 to 15, as said below
- out_weight: bfloat16 [8192, 8192], P('head'), may hold values from -1 to 1
Outputs:
- mixed: bfloat16 [4096, 8192], P(('ctx', 'head'))
The draws below stay inside these ranges and needn't reach their ends.
Inputs may be any that keep to these rules, and one draw needn't show every extreme that they name: `block_place`: A permutation of the block indices in which entries 2r and 2r + 1 sum to 15 and entry 2r is below 8.
All inputs are finite; a program needn't handle non-finite values.
Results may differ from the reference program's by a relative error of at most 0.015.
Values may be sent and summed in bfloat16 or wider, within the bound.
A program may use at most 128 MiB of HBM per device.

```python
import math
import jax
import jax.numpy as jnp
from jax import lax

HQ = 64
KVH = 8
DH = 128
D = 8192
BLK = 256
NBLOCK = 16
TOKENS = 4096
HEAD_DEV = 16
N_HEAD = 4


def draw_query(key, part):
    shape = (TOKENS, HQ, DH)
    result = jnp.clip(jax.random.normal(jax.random.fold_in(key, 1), shape, jnp.float32), -6.0, 6.0)
    return result.astype(jnp.bfloat16)


def draw_keys(key, part):
    shape = (TOKENS, KVH, DH)
    result = jnp.clip(jax.random.normal(jax.random.fold_in(key, 2), shape, jnp.float32), -6.0, 6.0)
    return result.astype(jnp.bfloat16)


def draw_block_place(key, part):
    shuffled = jax.random.permutation(jax.random.fold_in(key, 3), NBLOCK // 2).astype(jnp.int32)
    return jnp.stack([shuffled, NBLOCK - 1 - shuffled], axis=1).reshape(NBLOCK).astype(jnp.int32)


def block_scale(rng, shape, pieces, smallest, high):
    level, own = 1.0, jax.random.fold_in(rng, 6)
    for dim, blocks in pieces:
        draws = jnp.exp(jax.random.uniform(jax.random.fold_in(own, dim), (blocks,), jnp.float32, smallest / len(pieces), high / len(pieces)))
        level = level * jnp.repeat(draws, shape[dim] // blocks).reshape([-1 if axis == dim else 1 for axis in range(len(shape))])
    return level


def normal_values(stream_key, extent, spread, most, cuts=(), held_as=jnp.bfloat16):
    values = jax.random.normal(stream_key, extent, jnp.float32) * spread
    if len(cuts) > 0:
        values = block_scale(stream_key, extent, cuts, -0.22, 0.18) * values
    return jnp.clip(values, min=-most, max=most).astype(held_as)


def setup_inputs(seed: int = 0) -> dict:
    splits = jax.random.split(jax.random.key(seed), 8)
    query = draw_query(jax.random.fold_in(splits[7], 71), 0)
    keys = draw_keys(jax.random.fold_in(splits[7], 71), 0)
    values = normal_values(splits[2], (TOKENS, KVH, DH), 1.0, 6.0, ((0, 8), (1, 4)))
    k_scale = jnp.clip(jnp.exp(math.log(1.59375) - 0.98082925 * jax.random.uniform(splits[3], (NBLOCK, KVH), jnp.float32) ** block_scale(splits[3], (NBLOCK, KVH), ((0, 8), (1, 4)), -0.2, 0.2)), 0.59765625, 1.59375).astype(jnp.bfloat16)
    v_scale = jnp.clip(jnp.exp(math.log(2.0) - 1.3862944 * jax.random.uniform(splits[4], (NBLOCK, KVH), jnp.float32) ** block_scale(splits[4], (NBLOCK, KVH), ((0, 8), (1, 4)), -0.2, 0.2)), 0.5, 2.0).astype(jnp.bfloat16)
    block_place = draw_block_place(jax.random.fold_in(splits[7], 71), 0)
    out_weight = normal_values(splits[6], (HQ * DH, D), (HQ * DH // 256) ** -0.5, 1.0, ((0, 4),))
    return {"query": query, "keys": keys, "values": values, "k_scale": k_scale, "v_scale": v_scale, "block_place": block_place, "out_weight": out_weight}


masked_value = -1e+30

def reference(query, keys, values, k_scale, v_scale, block_place, out_weight):
    group_size = HQ // KVH
    inv_root = 1.0 / math.sqrt(DH)
    token_place = (block_place[:, None] * BLK + jnp.arange(BLK, dtype=jnp.int32)[None, :]).reshape(TOKENS).astype(jnp.int32)
    key_gain = jnp.repeat(k_scale.astype(jnp.float32), BLK, axis=0)
    value_gain = jnp.repeat(v_scale.astype(jnp.float32), BLK, axis=0)

    def one_block(item_index):
        block_id = item_index // KVH
        group_id = item_index % KVH
        picked = lax.dynamic_slice(query, (block_id * BLK, group_id * group_size, jnp.int32(0)), (BLK, group_size, DH)).astype(jnp.float32)
        key_rows = lax.dynamic_slice_in_dim(keys, group_id, 1, 1)[:, 0, :].astype(jnp.float32)
        value_rows = lax.dynamic_slice_in_dim(values, group_id, 1, 1)[:, 0, :].astype(jnp.float32)
        key_column = lax.dynamic_slice_in_dim(key_gain, group_id, 1, 1)[:, 0]
        value_column = lax.dynamic_slice_in_dim(value_gain, group_id, 1, 1)[:, 0]
        scores = jnp.einsum('qrd,kd->rqk', picked, key_rows, precision=lax.Precision.HIGHEST)
        scores = scores * (key_column * inv_root)[None, None, :]
        query_place = lax.dynamic_slice_in_dim(token_place, block_id * BLK, BLK)
        visible = query_place[:, None] >= token_place[None, :]
        scores = jnp.where(visible[None], scores, masked_value)
        largest = lax.optimization_barrier(jnp.max(scores, axis=-1, keepdims=True))
        weights = jnp.exp(scores - largest)
        totals = lax.optimization_barrier(jnp.sum(weights, axis=-1))
        rounded = lax.optimization_barrier(weights.astype(jnp.bfloat16)).astype(jnp.float32)
        scaled_values = value_rows * value_column[:, None]
        summed = jnp.einsum('rqk,kd->rqd', rounded, scaled_values, precision=lax.Precision.HIGHEST)
        return (summed / totals[..., None]).astype(jnp.bfloat16)
    blocks = lax.map(one_block, jnp.arange(NBLOCK * KVH, dtype=jnp.int32))
    attended = blocks.reshape(NBLOCK, KVH, group_size, BLK, DH).transpose(0, 3, 1, 2, 4).reshape(TOKENS, HQ * DH)
    slab_width = HEAD_DEV * DH

    def add_group(running, group_index):
        part_rows = lax.dynamic_slice_in_dim(attended, group_index * slab_width, slab_width, 1)
        part_weight = lax.dynamic_slice_in_dim(out_weight, group_index * slab_width, slab_width, 0)
        group_term = jnp.dot(part_rows, part_weight, preferred_element_type=jnp.float32)
        rounded_term = lax.optimization_barrier(group_term.astype(jnp.bfloat16))
        return (running + rounded_term.astype(jnp.float32), None)
    summed_all, unused = lax.scan(add_group, jnp.zeros((TOKENS, D), jnp.float32), jnp.arange(N_HEAD, dtype=jnp.int32))
    return summed_all.astype(jnp.bfloat16)
```

```python
import functools
import math

import jax
import jax.numpy as jnp
from jax import lax
from jax.experimental import pallas as pl
from jax.experimental.pallas import tpu as pltpu
from jax.sharding import PartitionSpec as P

masked_value = -1e30
COLUMN_STEP = 512
LAG = 3


def attend_kernel(
    per_group, block_len, head_dim, blocks, first_slot, later,
    order, own, key_gain, value_gain,
    q_ref, k_ref, vt_ref, *refs,
):
    group = pl.program_id(0)
    query_ref = refs[-1]
    if later:
        old_max, old_total, old_sum, o_ref, max_ref, total_ref, sum_ref = refs[:-1]
    elif first_slot == 0:
        o_ref, max_ref, total_ref, sum_ref = refs[:-1]
    else:
        max_ref, total_ref, sum_ref = refs[:-1]
    place = own[first_slot]
    for h in range(per_group):
        query_ref[h] = q_ref[:, h * head_dim : (h + 1) * head_dim].T

    def visit(indices, diagonal):
        found = [order[index] for index in indices]
        keys = [k_ref[lax.div(block, 2)] for block in found]
        values = [vt_ref[lax.div(block, 2)] for block in found]
        gains = [key_gain[group * blocks + block] for block in found]
        scales = [value_gain[group * blocks + block] for block in found]
        if diagonal:
            shape = (block_len, block_len)
            visible = lax.broadcasted_iota(jnp.int32, shape, 0) <= lax.broadcasted_iota(
                jnp.int32, shape, 1
            )

        def score(h):
            result = [
                jnp.dot(key, query_ref[h], preferred_element_type=jnp.float32) for key in keys
            ]
            if diagonal:
                result[-1] = jnp.where(visible, result[-1], masked_value)
            return result

        def weigh(h, scores):
            old = max_ref[h : h + 1, :]
            top = old
            for part, gain in zip(scores, gains):
                top = jnp.maximum(top, jnp.max(part, axis=0, keepdims=True) * gain)
            factor = jnp.exp2(old - top)
            total = factor * total_ref[h : h + 1, :]
            rounded = []
            for part, gain in zip(scores, gains):
                weights = jnp.exp2(part * gain - top)
                total = total + jnp.sum(weights, axis=0, keepdims=True)
                rounded.append(weights.astype(jnp.bfloat16))
            max_ref[h : h + 1, :] = top
            total_ref[h : h + 1, :] = total
            return rounded, factor

        def gather(h, rounded, factor):
            running = factor * sum_ref[h]
            for part, value, scale in zip(rounded, values, scales):
                running = running + scale * jnp.dot(
                    value, part, preferred_element_type=jnp.float32
                )
            sum_ref[h] = running

        scores = score(0)
        waiting = None
        for h in range(per_group):
            upcoming = score(h + 1) if h + 1 < per_group else None
            if waiting is not None:
                gather(h - 1, *waiting)
            waiting = weigh(h, scores)
            scores = upcoming
        gather(per_group - 1, *waiting)

    half = blocks // 2
    if later:
        max_ref[...] = old_max[...]
        total_ref[...] = old_total[...]
        sum_ref[...] = old_sum[...]
        start, stop = half, place
    else:
        max_ref[...] = jnp.full(max_ref.shape, masked_value, jnp.float32)
        total_ref[...] = jnp.zeros(total_ref.shape, jnp.float32)
        sum_ref[...] = jnp.zeros(sum_ref.shape, jnp.float32)
        start, stop = 0, (place if first_slot == 0 else half)
    pairs = (stop - start) // 2

    @pl.loop(0, pairs)
    def _(pair):
        visit([start + 2 * pair, start + 2 * pair + 1], False)

    if later or first_slot == 0:
        odd = (stop - start) - 2 * pairs

        @pl.when(odd == 1)
        def _():
            visit([place - 1, place], True)

        @pl.when(odd == 0)
        def _():
            visit([place], True)

        for h in range(per_group):
            columns = slice(h * head_dim, (h + 1) * head_dim)
            mean = sum_ref[h] / total_ref[h : h + 1, :]
            o_ref[:, columns] = mean.T.astype(o_ref.dtype)
    elif half % 2:
        visit([half - 1], False)


def attend(facts, query, gathered, group_count, head_dim, slot, state=None):
    rows, width = query.shape
    devices = gathered.shape[0]
    block_len = rows // 2
    group_width = width // group_count
    per_group = group_width // head_dim
    heads = group_count * per_group
    blocks = facts[0].shape[0]
    later = state is not None
    tiles = blocks // 4 if later or slot == 0 else blocks // 2
    pairs = tiles * block_len * block_len * heads
    row_spec = pl.BlockSpec((per_group, block_len), lambda g, *_: (g, 0))
    sum_spec = pl.BlockSpec((per_group, head_dim, block_len), lambda g, *_: (g, 0, 0))
    state_specs = [row_spec, row_spec, sum_spec]
    row_shape = (per_group, block_len)
    sum_shape = (per_group, head_dim, block_len)
    first_value = block_len // head_dim
    outs = ([pl.BlockSpec((block_len, group_width), lambda g, *_: (0, g))],
            [jax.ShapeDtypeStruct((block_len, width), jnp.bfloat16)])
    scratch = [
        pltpu.VMEM(row_shape, jnp.float32),
        pltpu.VMEM(row_shape, jnp.float32),
        pltpu.VMEM(sum_shape, jnp.float32),
    ]
    if not later and slot == 1:
        outs = (state_specs, [
            jax.ShapeDtypeStruct((heads, block_len), jnp.float32),
            jax.ShapeDtypeStruct((heads, block_len), jnp.float32),
            jax.ShapeDtypeStruct((heads, head_dim, block_len), jnp.float32),
        ])
        scratch = []
    scratch.append(pltpu.VMEM((per_group, head_dim, block_len), jnp.bfloat16))
    results = pl.pallas_call(
        functools.partial(
            attend_kernel, per_group, block_len, head_dim, blocks, slot, later
        ),
        grid_spec=pltpu.PrefetchScalarGridSpec(
            num_scalar_prefetch=4,
            grid=(group_count,),
            in_specs=[
                pl.BlockSpec((block_len, group_width), lambda g, *_: (slot, g)),
                pl.BlockSpec((devices, block_len, head_dim), lambda g, *_: (0, 0, g)),
                pl.BlockSpec(
                    (devices, head_dim, block_len), lambda g, *_: (0, first_value + g, 0)
                ),
            ] + (state_specs if later else []),
            out_specs=outs[0],
            scratch_shapes=scratch,
        ),
        out_shape=outs[1],
        compiler_params=pltpu.CompilerParams(vmem_limit_bytes=40 * 1024 * 1024),
        cost_estimate=pl.CostEstimate(
            flops=4 * pairs * head_dim, bytes_accessed=4 << 20, transcendentals=pairs
        ),
    )(*facts, query, gathered, gathered, *(state if later else ()))
    return results if len(results) > 1 else results[0]


def gather_attend_kernel(
    rate, per_group, head_dim,
    own_ref, own_facts, q_ref, o_ref,
    kv, facts, query_ref, max_ref, total_ref, sum_ref,
    recv, send_right, send_left, send_beside,
):
    groups = kv.shape[1] // 2
    units = kv.shape[1]
    block_len = kv.shape[2]
    chips = kv.shape[0] // 2
    me = lax.axis_index("ctx")
    z, core = me // 2, me % 2
    beside = 2 * z + 1 - core
    half = z // 2
    middle = (z % 2 + half) % 2
    first = z + 1 - 2 * (z % 2)
    second = 2 - half
    third = 3 * (1 - half)

    barrier = pltpu.get_barrier_semaphore()

    def greet(device):
        pl.semaphore_signal(
            barrier, inc=1, device_id={"ctx": device}, device_id_type=pl.DeviceIdType.MESH
        )

    greet(beside)

    @pl.when(z > 0)
    def _():
        greet(me - 2)

    @pl.when(z < chips - 1)
    def _():
        greet(me + 2)

    for unit in range(units):
        kv[me, unit] = own_ref[unit]
    facts[me] = own_facts[...]

    @pl.when((z > 0) & (z < chips - 1))
    def _():
        pl.semaphore_wait(barrier, 3)

    @pl.when((z == 0) | (z == chips - 1))
    def _():
        pl.semaphore_wait(barrier, 2)

    def move(origin, unit, sems, target):
        return pltpu.make_async_remote_copy(
            src_ref=kv.at[origin, unit], dst_ref=kv.at[origin, unit],
            send_sem=sems.at[origin // 2, unit], recv_sem=recv.at[origin, unit],
            device_id={"ctx": target}, device_id_type=pl.DeviceIdType.MESH,
        )

    def move_facts(origin, sems, target):
        return pltpu.make_async_remote_copy(
            src_ref=facts.at[origin], dst_ref=facts.at[origin],
            send_sem=sems.at[origin // 2, units], recv_sem=recv.at[origin, units],
            device_id={"ctx": target}, device_id_type=pl.DeviceIdType.MESH,
        )

    def send_own(sems, target):
        move_facts(me, sems, target).start()
        for unit in range(units):
            move(me, unit, sems, target).start()

    @pl.when(z < chips - 1)
    def _():
        send_own(send_right, me + 2)

    @pl.when(z > 0)
    def _():
        send_own(send_left, me - 2)

    send_own(send_beside, beside)

    def on(chip, action):
        action(send_beside, beside)

        @pl.when((chip < z) & (z < chips - 1))
        def _():
            action(send_right, me + 2)

        @pl.when((chip > z) & (z > 0))
        def _():
            action(send_left, me - 2)

    def pass_on(chip, unit, with_facts):
        origin = 2 * chip + core
        move(origin, unit, send_beside, beside).wait_recv()
        on(chip, lambda sems, target: move(origin, unit, sems, target).start())

        @pl.when(with_facts)
        def _():
            move_facts(origin, send_beside, beside).wait_recv()
            on(chip, lambda sems, target: move_facts(origin, sems, target).start())

    def arrive(origin, unit):
        move(origin, unit, send_beside, beside).wait_recv()

    def arrive_facts(origin):
        move_facts(origin, send_beside, beside).wait_recv()

    max_ref[...] = jnp.full(max_ref.shape, masked_value, jnp.float32)
    total_ref[...] = jnp.zeros(total_ref.shape, jnp.float32)
    sum_ref[...] = jnp.zeros(sum_ref.shape, jnp.float32)

    for g in range(groups):
        for h in range(per_group):
            columns = slice((g * per_group + h) * head_dim, (g * per_group + h + 1) * head_dim)
            for row in range(2):
                query_ref[row, g, h] = q_ref[row * block_len : (row + 1) * block_len, columns].T

    def gain_row(origin, slot, g):
        low = facts[origin, slot * groups : (slot + 1) * groups, :].astype(jnp.float32)
        row = low[0:1, :]
        for other in range(1, groups):
            row = jnp.where(g == other, low[other : other + 1, :], row)
        return row * rate

    def scale_row(origin, slot, g):
        base = 2 * groups + slot * groups
        low = facts[origin, base : base + groups, :].astype(jnp.float32)
        row = low[0:1, :]
        for other in range(1, groups):
            row = jnp.where(g == other, low[other : other + 1, :], row)
        return row

    def place_row(origin):
        return facts[origin, 4 * groups : 4 * groups + 1, :].astype(jnp.float32)

    def visit(parts, row, g, diagonal=False, blend=None):
        turned = [(key, value.T, gain, scale) for key, value, gain, scale in parts]
        if diagonal:
            shape = (block_len, block_len)
            visible = lax.broadcasted_iota(jnp.int32, shape, 0) <= lax.broadcasted_iota(
                jnp.int32, shape, 1
            )
        if blend is not None:
            is_low, low_share, high_share = blend

        def held(ref, index):
            if blend is None:
                return ref[(row, g) + index]
            return jnp.where(is_low, ref[(0, g) + index], ref[(1, g) + index])

        def keep(ref, index, value):
            if blend is None:
                ref[(row, g) + index] = value
            else:
                ref[(0, g) + index] = jnp.where(is_low, value, ref[(0, g) + index])
                ref[(1, g) + index] = jnp.where(is_low, ref[(1, g) + index], value)

        def score(h):
            if blend is None:
                query = query_ref[row, g, h]
            else:
                query = query_ref[0, g, h] * low_share + query_ref[1, g, h] * high_share
            result = [
                jnp.dot(key, query, preferred_element_type=jnp.float32) for key, _, _, _ in turned
            ]
            if diagonal:
                result[-1] = jnp.where(visible, result[-1], masked_value)
            return result

        def weigh(h, scores):
            line = (slice(h, h + 1), slice(None))
            old = held(max_ref, line)
            top = old
            for part, (_, _, gain, _) in zip(scores, turned):
                top = jnp.maximum(top, jnp.max(part, axis=0, keepdims=True) * gain)
            factor = jnp.exp2(old - top)
            total = factor * held(total_ref, line)
            rounded = []
            for part, (_, _, gain, _) in zip(scores, turned):
                weights = jnp.exp2(part * gain - top)
                total = total + jnp.sum(weights, axis=0, keepdims=True)
                rounded.append(weights.astype(jnp.bfloat16))
            keep(max_ref, line, top)
            keep(total_ref, line, total)
            return rounded, factor

        def gather(h, rounded, factor):
            running = factor * held(sum_ref, (h,))
            for part, (_, value, _, scale) in zip(rounded, turned):
                running = running + scale * jnp.dot(
                    value, part, preferred_element_type=jnp.float32
                )
            keep(sum_ref, (h,), running)

        scores = score(0)
        waiting = None
        for h in range(per_group):
            upcoming = score(h + 1) if h + 1 < per_group else None
            if waiting is not None:
                gather(h - 1, *waiting)
            waiting = weigh(h, scores)
            scores = upcoming
        gather(per_group - 1, *waiting)

    def part_of(origin, slot, g):
        unit = slot * groups + g
        return (
            kv[origin, unit, :, :head_dim], kv[origin, unit, :, head_dim:],
            gain_row(origin, slot, g), scale_row(origin, slot, g),
        )

    def visit_picked(origin, g):
        is_low = place_row(origin) < place_row(me)
        low_share = is_low.astype(jnp.float32)
        high_share = 1.0 - low_share
        low, high = part_of(origin, 0, g), part_of(origin, 1, g)
        low_bits, high_bits = low_share.astype(jnp.bfloat16), high_share.astype(jnp.bfloat16)
        narrow = (slice(None), slice(0, head_dim))
        part = (
            low[0] * low_bits[narrow] + high[0] * high_bits[narrow],
            low[1] * low_bits[narrow] + high[1] * high_bits[narrow],
            jnp.where(is_low, low[2], high[2]),
            jnp.where(is_low, low[3], high[3]),
        )
        visit([part], None, g, blend=(is_low, low_bits, high_bits))

    def pass_near(unit):
        pass_on(first, unit, unit == 0)

        @pl.when(middle == 1)
        def _():
            pass_on(second, unit, unit == 0)

    @pl.loop(0, groups)
    def _(g):
        visit([part_of(me, 0, g)], 0, g, diagonal=True)
        pass_near(g)

    @pl.loop(0, groups)
    def _(g):
        visit([part_of(me, 1, g)], 1, g, diagonal=True)
        pass_near(groups + g)

    def attend_chip(chip):
        def pair(g):
            visit([part_of(2 * chip, 0, g), part_of(2 * chip + 1, 0, g)], 1, g)

        return pair

    @pl.loop(0, groups)
    def _(g):
        arrive(beside, g)

        @pl.when(g == 0)
        def _():
            arrive_facts(beside)

        attend_chip(z)(g)

    @pl.loop(0, groups)
    def _(g):
        arrive(beside, groups + g)
        visit_picked(beside, g)

    @pl.loop(0, chips - 1)
    def _(j):
        chip = first * ((1 - j) * (2 - j) // 2) + second * (j * (2 - j)) + third * (j * (j - 1) // 2)
        step = middle + j - 1
        passing = second + (third - second) * step

        @pl.loop(0, groups)
        def _(g):
            @pl.when((j >= 1) & (step <= 1))
            def _():
                pass_on(passing, g, g == 0)

            arrive(2 * chip + 1 - core, g)

            @pl.when(g == 0)
            def _():
                arrive_facts(2 * chip + 1 - core)

            attend_chip(chip)(g)

        @pl.loop(0, groups)
        def _(g):
            @pl.when((j >= 1) & (step <= 1))
            def _():
                pass_on(passing, groups + g, False)

            visit_picked(2 * chip + core, g)
            arrive(2 * chip + 1 - core, groups + g)
            visit_picked(2 * chip + 1 - core, g)

    @pl.loop(0, 2)
    def _(row):
        rows = pl.ds(pl.multiple_of(row * block_len, block_len), block_len)
        for g in range(groups):
            for h in range(per_group):
                start = (g * per_group + h) * head_dim
                mean = sum_ref[row, g, h] / total_ref[row, g, h : h + 1, :]
                o_ref[rows, start : start + head_dim] = mean.astype(o_ref.dtype).T

    def sent(origin, sems, target):
        move_facts(origin, sems, target).wait_send()
        for unit in range(units):
            move(origin, unit, sems, target).wait_send()

    @pl.when(z < chips - 1)
    def _():
        sent(me, send_right, me + 2)

    @pl.when(z > 0)
    def _():
        sent(me, send_left, me - 2)

    sent(me, send_beside, beside)

    @pl.loop(0, chips)
    def _(chip):
        @pl.when(chip != z)
        def _():
            on(chip, lambda sems, target: sent(2 * chip + core, sems, target))


def gather_attend(query, keys, values, k_scale, v_scale, block_place):
    rows, head_count, head_dim = query.shape
    groups = keys.shape[1]
    slots = block_place.shape[0]
    block_len = rows // slots
    devices = lax.axis_size("ctx")
    chips = devices // 2
    units = slots * groups
    per_group = head_count // groups
    width = 2 * head_dim
    own = jnp.concatenate([keys, values], axis=2).reshape(slots, block_len, groups, width)
    own = own.transpose(0, 2, 1, 3).reshape(units, block_len, width)
    listed = jnp.concatenate(
        [k_scale.reshape(-1), v_scale.reshape(-1), block_place[:1].astype(jnp.bfloat16)]
    )
    listed = jnp.pad(listed, (0, 16 - listed.shape[0]))
    own_facts = jnp.broadcast_to(listed[:, None], (16, width))
    state = (2, groups, per_group)
    tiles = 2 * devices + 1
    pairs = tiles * block_len * block_len * head_count
    whole = pl.BlockSpec(memory_space=pltpu.VMEM)
    return pl.pallas_call(
        functools.partial(
            gather_attend_kernel, math.log2(math.e) / math.sqrt(head_dim), per_group, head_dim
        ),
        in_specs=[whole] * 3,
        out_specs=whole,
        scratch_shapes=[
            pltpu.VMEM((devices, units, block_len, width), jnp.bfloat16),
            pltpu.VMEM((devices, 16, width), jnp.bfloat16),
            pltpu.VMEM(state + (head_dim, block_len), jnp.bfloat16),
            pltpu.VMEM(state + (block_len,), jnp.float32),
            pltpu.VMEM(state + (block_len,), jnp.float32),
            pltpu.VMEM(state + (head_dim, block_len), jnp.float32),
            pltpu.SemaphoreType.DMA((devices, units + 1)),
            pltpu.SemaphoreType.DMA((chips, units + 1)),
            pltpu.SemaphoreType.DMA((chips, units + 1)),
            pltpu.SemaphoreType.DMA((chips, units + 1)),
        ],
        out_shape=jax.ShapeDtypeStruct((rows, head_count * head_dim), jnp.bfloat16),
        compiler_params=pltpu.CompilerParams(
            collective_id=1, has_side_effects=True, vmem_limit_bytes=40 * 1024 * 1024
        ),
        cost_estimate=pl.CostEstimate(
            flops=4 * pairs * head_dim, bytes_accessed=8 << 20, transcendentals=pairs
        ),
    )(own, own_facts, query.reshape(rows, head_count * head_dim))


def project_kernel(
    chunks,
    low_ref, high_ref, w_ref, o_ref,
    lhs, sent, kept, arrived, passed, ended,
    send_one, recv_one, send_two, recv_two,
):
    t = pl.program_id(0)
    me = lax.axis_index("head")
    along_x = me + 1 - 2 * (me % 2)
    along_y = (me + 2) % 4
    part = low_ref.shape[0] // 2

    @pl.when(t == 0)
    def _():
        barrier = pltpu.get_barrier_semaphore()
        for partner in (along_x, along_y):
            pl.semaphore_signal(
                barrier, inc=1, device_id={"head": partner},
                device_id_type=pl.DeviceIdType.MESH,
            )
        for parity in range(2):
            near, far = (along_x, along_y) if parity == 0 else (along_y, along_x)
            for slot, owner in enumerate((3 - me, near, far, me)):
                rows = pl.ds(pl.multiple_of((owner % 2) * part, part), part)

                @pl.when(owner // 2 == 0)
                def _():
                    lhs[parity, slot * part : (slot + 1) * part, :] = low_ref[rows, :]

                @pl.when(owner // 2 == 1)
                def _():
                    lhs[parity, slot * part : (slot + 1) * part, :] = high_ref[rows, :]

        pl.semaphore_wait(barrier, 2)

    def first_copy(c):
        near = along_x + (c % 2) * (along_y - along_x)
        return pltpu.make_async_remote_copy(
            src_ref=sent.at[c], dst_ref=arrived.at[c],
            send_sem=send_one.at[c], recv_sem=recv_one.at[c],
            device_id={"head": near}, device_id_type=pl.DeviceIdType.MESH,
        )

    def second_copy(c):
        far = along_y + (c % 2) * (along_x - along_y)
        return pltpu.make_async_remote_copy(
            src_ref=passed.at[c], dst_ref=ended.at[c],
            send_sem=send_two.at[c], recv_sem=recv_two.at[c],
            device_id={"head": far}, device_id_type=pl.DeviceIdType.MESH,
        )

    @pl.when(t < chunks)
    def _():
        term = jnp.dot(lhs[t % 2], w_ref[...], preferred_element_type=jnp.float32)
        term = term.astype(jnp.bfloat16)
        sent[t] = term[: 2 * part]
        kept[t] = term[2 * part :]
        first_copy(t).start()

    @pl.when((t >= LAG) & (t < chunks + LAG))
    def _():
        c = t - LAG
        first_copy(c).wait()
        passed[c] = (
            arrived[c, :part, :].astype(jnp.float32) + kept[c, :part, :].astype(jnp.float32)
        ).astype(jnp.bfloat16)
        second_copy(c).start()

    @pl.when(t >= 2 * LAG)
    def _():
        c = t - 2 * LAG
        second_copy(c).wait()
        o_ref[...] = (
            arrived[c, part:, :].astype(jnp.float32)
            + kept[c, part:, :].astype(jnp.float32)
            + ended[c].astype(jnp.float32)
        ).astype(jnp.bfloat16)


def project(attended, weight):
    depth, columns = weight.shape
    rows = attended.shape[0]
    part = rows // 4
    step = COLUMN_STEP
    chunks = columns // step
    last = chunks - 1
    return pl.pallas_call(
        functools.partial(project_kernel, chunks),
        grid_spec=pltpu.PrefetchScalarGridSpec(
            num_scalar_prefetch=0,
            grid=(chunks + 2 * LAG,),
            in_specs=[
                pl.BlockSpec((rows // 2, depth), lambda t: (0, 0)),
                pl.BlockSpec((rows // 2, depth), lambda t: (1, 0)),
                pl.BlockSpec((depth, step), lambda t: (0, jnp.minimum(t, last))),
            ],
            out_specs=pl.BlockSpec((part, step), lambda t: (0, jnp.maximum(t - 2 * LAG, 0))),
            scratch_shapes=[
                pltpu.VMEM((2, rows, depth), jnp.bfloat16),
                pltpu.VMEM((chunks, 2 * part, step), jnp.bfloat16),
                pltpu.VMEM((chunks, 2 * part, step), jnp.bfloat16),
                pltpu.VMEM((chunks, 2 * part, step), jnp.bfloat16),
                pltpu.VMEM((chunks, part, step), jnp.bfloat16),
                pltpu.VMEM((chunks, part, step), jnp.bfloat16),
                pltpu.SemaphoreType.DMA((chunks,)),
                pltpu.SemaphoreType.DMA((chunks,)),
                pltpu.SemaphoreType.DMA((chunks,)),
                pltpu.SemaphoreType.DMA((chunks,)),
            ],
        ),
        out_shape=jax.ShapeDtypeStruct((part, columns), jnp.bfloat16),
        compiler_params=pltpu.CompilerParams(
            collective_id=0, has_side_effects=True, vmem_limit_bytes=56 * 1024 * 1024
        ),
        cost_estimate=pl.CostEstimate(
            flops=2 * rows * depth * columns, bytes_accessed=2 * depth * columns,
            transcendentals=0,
        ),
    )(attended, attended, weight)


def body(query, keys, values, k_scale, v_scale, block_place, out_weight):
    rows, head_count, head_dim = query.shape
    group_count = keys.shape[1]
    slots = block_place.shape[0]
    devices = lax.axis_size("ctx")
    blocks = slots * devices
    block_len = rows // slots
    if lax.axis_size("head") == 4 and devices == 8 and slots == 2 and block_len == 2 * head_dim:
        mixed_heads = gather_attend(query, keys, values, k_scale, v_scale, block_place)
        return project(mixed_heads, out_weight)
    width = group_count * head_dim
    facts = jnp.concatenate(
        [k_scale, v_scale, block_place[:, None].astype(jnp.bfloat16)], axis=1
    )
    facts = jnp.pad(facts, ((0, 16 - slots), (0, block_len - facts.shape[1])))

    def payload(slot):
        part = slice(slot * block_len, (slot + 1) * block_len)
        key = keys[part].reshape(block_len, width)
        key = jnp.pad(key, ((0, 0), (0, block_len - width))) if width < block_len else key
        return [key, values[part].reshape(block_len, width).T]

    low_part = lax.all_gather(jnp.concatenate(payload(0) + [facts]), "ctx", axis=0)
    high_part = lax.all_gather(jnp.concatenate(payload(1)), "ctx", axis=0)
    base = block_len + width
    all_facts = low_part[:, base : base + slots, : 2 * group_count + 1].reshape(blocks, -1)
    all_facts = all_facts.astype(jnp.float32)
    places = all_facts[:, -1].astype(jnp.int32)
    ids = jnp.arange(blocks, dtype=jnp.int32)
    order = jnp.sum(jnp.where(places[None, :] == ids[:, None], ids[None, :], 0), axis=1)
    rate = math.log2(math.e) / math.sqrt(head_dim)
    key_gain = (all_facts[:, :group_count] * rate).T.reshape(-1)
    value_gain = all_facts[:, group_count : 2 * group_count].T.reshape(-1)
    known = (order, block_place, key_gain, value_gain)
    flat = query.reshape(rows, head_count * head_dim)
    state = attend(known, flat, low_part, group_count, head_dim, 1)
    low = attend(known, flat, low_part, group_count, head_dim, 0)
    high = attend(known, flat, high_part, group_count, head_dim, 1, state)
    term = jnp.dot(jnp.concatenate([low, high]), out_weight, preferred_element_type=jnp.float32)
    return lax.psum_scatter(
        term.astype(jnp.bfloat16), "head", scatter_dimension=0, tiled=True
    )


def solution(mesh):
    placed = (
        P("ctx", "head", None),
        P("ctx", "head", None),
        P("ctx", "head", None),
        P("ctx", "head"),
        P("ctx", "head"),
        P("ctx"),
        P("head", None),
    )
    return jax.shard_map(
        body, mesh=mesh, in_specs=placed, out_specs=P(("ctx", "head"), None), check_vma=False
    )
```

```python
import functools
import math

import jax
import jax.numpy as jnp
from jax import lax
from jax.experimental import pallas as pl
from jax.experimental.pallas import tpu as pltpu
from jax.sharding import PartitionSpec as P

masked_value = -1e30
COLUMN_STEP = 512
LAG = 3


def attend_kernel(
    per_group, block_len, head_dim, blocks, first_slot, later,
    order, own, key_gain, value_gain,
    q_ref, k_ref, vt_ref, *refs,
):
    group = pl.program_id(0)
    query_ref = refs[-1]
    if later:
        old_max, old_total, old_sum, o_ref, max_ref, total_ref, sum_ref = refs[:-1]
    elif first_slot == 0:
        o_ref, max_ref, total_ref, sum_ref = refs[:-1]
    else:
        max_ref, total_ref, sum_ref = refs[:-1]
    place = own[first_slot]
    for h in range(per_group):
        query_ref[h] = q_ref[:, h * head_dim : (h + 1) * head_dim].T

    def visit(indices, diagonal):
        found = [order[index] for index in indices]
        keys = [k_ref[lax.div(block, 2)] for block in found]
        values = [vt_ref[lax.div(block, 2)] for block in found]
        gains = [key_gain[group * blocks + block] for block in found]
        scales = [value_gain[group * blocks + block] for block in found]
        if diagonal:
            shape = (block_len, block_len)
            visible = lax.broadcasted_iota(jnp.int32, shape, 0) <= lax.broadcasted_iota(
                jnp.int32, shape, 1
            )

        def score(h):
            result = [
                jnp.dot(key, query_ref[h], preferred_element_type=jnp.float32) for key in keys
            ]
            if diagonal:
                result[-1] = jnp.where(visible, result[-1], masked_value)
            return result

        def weigh(h, scores):
            old = max_ref[h : h + 1, :]
            top = old
            for part, gain in zip(scores, gains):
                top = jnp.maximum(top, jnp.max(part, axis=0, keepdims=True) * gain)
            factor = jnp.exp2(old - top)
            total = factor * total_ref[h : h + 1, :]
            rounded = []
            for part, gain in zip(scores, gains):
                weights = jnp.exp2(part * gain - top)
                total = total + jnp.sum(weights, axis=0, keepdims=True)
                rounded.append(weights.astype(jnp.bfloat16))
            max_ref[h : h + 1, :] = top
            total_ref[h : h + 1, :] = total
            return rounded, factor

        def gather(h, rounded, factor):
            running = factor * sum_ref[h]
            for part, value, scale in zip(rounded, values, scales):
                running = running + scale * jnp.dot(
                    value, part, preferred_element_type=jnp.float32
                )
            sum_ref[h] = running

        scores = score(0)
        waiting = None
        for h in range(per_group):
            upcoming = score(h + 1) if h + 1 < per_group else None
            if waiting is not None:
                gather(h - 1, *waiting)
            waiting = weigh(h, scores)
            scores = upcoming
        gather(per_group - 1, *waiting)

    half = blocks // 2
    if later:
        max_ref[...] = old_max[...]
        total_ref[...] = old_total[...]
        sum_ref[...] = old_sum[...]
        start, stop = half, place
    else:
        max_ref[...] = jnp.full(max_ref.shape, masked_value, jnp.float32)
        total_ref[...] = jnp.zeros(total_ref.shape, jnp.float32)
        sum_ref[...] = jnp.zeros(sum_ref.shape, jnp.float32)
        start, stop = 0, (place if first_slot == 0 else half)
    pairs = (stop - start) // 2

    @pl.loop(0, pairs)
    def _(pair):
        visit([start + 2 * pair, start + 2 * pair + 1], False)

    if later or first_slot == 0:
        odd = (stop - start) - 2 * pairs

        @pl.when(odd == 1)
        def _():
            visit([place - 1, place], True)

        @pl.when(odd == 0)
        def _():
            visit([place], True)

        for h in range(per_group):
            columns = slice(h * head_dim, (h + 1) * head_dim)
            mean = sum_ref[h] / total_ref[h : h + 1, :]
            o_ref[:, columns] = mean.T.astype(o_ref.dtype)
    elif half % 2:
        visit([half - 1], False)


def attend(facts, query, gathered, group_count, head_dim, slot, state=None):
    rows, width = query.shape
    devices = gathered.shape[0]
    block_len = rows // 2
    group_width = width // group_count
    per_group = group_width // head_dim
    heads = group_count * per_group
    blocks = facts[0].shape[0]
    later = state is not None
    tiles = blocks // 4 if later or slot == 0 else blocks // 2
    pairs = tiles * block_len * block_len * heads
    row_spec = pl.BlockSpec((per_group, block_len), lambda g, *_: (g, 0))
    sum_spec = pl.BlockSpec((per_group, head_dim, block_len), lambda g, *_: (g, 0, 0))
    state_specs = [row_spec, row_spec, sum_spec]
    row_shape = (per_group, block_len)
    sum_shape = (per_group, head_dim, block_len)
    first_value = block_len // head_dim
    outs = ([pl.BlockSpec((block_len, group_width), lambda g, *_: (0, g))],
            [jax.ShapeDtypeStruct((block_len, width), jnp.bfloat16)])
    scratch = [
        pltpu.VMEM(row_shape, jnp.float32),
        pltpu.VMEM(row_shape, jnp.float32),
        pltpu.VMEM(sum_shape, jnp.float32),
    ]
    if not later and slot == 1:
        outs = (state_specs, [
            jax.ShapeDtypeStruct((heads, block_len), jnp.float32),
            jax.ShapeDtypeStruct((heads, block_len), jnp.float32),
            jax.ShapeDtypeStruct((heads, head_dim, block_len), jnp.float32),
        ])
        scratch = []
    scratch.append(pltpu.VMEM((per_group, head_dim, block_len), jnp.bfloat16))
    results = pl.pallas_call(
        functools.partial(
            attend_kernel, per_group, block_len, head_dim, blocks, slot, later
        ),
        grid_spec=pltpu.PrefetchScalarGridSpec(
            num_scalar_prefetch=4,
            grid=(group_count,),
            in_specs=[
                pl.BlockSpec((block_len, group_width), lambda g, *_: (slot, g)),
                pl.BlockSpec((devices, block_len, head_dim), lambda g, *_: (0, 0, g)),
                pl.BlockSpec(
                    (devices, head_dim, block_len), lambda g, *_: (0, first_value + g, 0)
                ),
            ] + (state_specs if later else []),
            out_specs=outs[0],
            scratch_shapes=scratch,
        ),
        out_shape=outs[1],
        compiler_params=pltpu.CompilerParams(vmem_limit_bytes=40 * 1024 * 1024),
        cost_estimate=pl.CostEstimate(
            flops=4 * pairs * head_dim, bytes_accessed=4 << 20, transcendentals=pairs
        ),
    )(*facts, query, gathered, gathered, *(state if later else ()))
    return results if len(results) > 1 else results[0]


def mix_kernel(
    rate, per_group, head_dim, chunks,
    block_place, own_ref, own_k_scale, own_v_scale, q_ref, w_ref, o_ref,
    kv, facts, query_ref, max_ref, total_ref, sum_ref,
    attended, held_w, terms, arrived, passed, ended,
    recv, send_right, send_left, send_beside,
    load_w, send_one, recv_one, send_two, recv_two,
):
    groups = kv.shape[1] // 2
    units = kv.shape[1]
    block_len = kv.shape[2]
    chips = kv.shape[0] // 2
    me = lax.axis_index("ctx")
    z, core = me // 2, me % 2
    beside = 2 * z + 1 - core
    half = z // 2
    middle = (z % 2 + half) % 2
    first = z + 1 - 2 * (z % 2)
    second = 2 - half
    third = 3 * (1 - half)

    head = lax.axis_index("head")
    along_x = head + 1 - 2 * (head % 2)
    along_y = (head + 2) % 4
    step_columns = held_w.shape[2]
    part = o_ref.shape[0]

    def fetch(chunk):
        columns = pl.ds(pl.multiple_of(chunk * step_columns, step_columns), step_columns)
        return pltpu.make_async_copy(
            w_ref.at[:, columns], held_w.at[chunk % 3], load_w.at[chunk % 3]
        )

    fetch(0).start()
    fetch(1).start()

    barrier = pltpu.get_barrier_semaphore()

    def greet(device):
        pl.semaphore_signal(
            barrier, inc=1, device_id={"ctx": device}, device_id_type=pl.DeviceIdType.MESH
        )

    for partner in (along_x, along_y):
        pl.semaphore_signal(
            barrier, inc=1, device_id={"head": partner}, device_id_type=pl.DeviceIdType.MESH
        )
    greet(beside)

    @pl.when(z > 0)
    def _():
        greet(me - 2)

    @pl.when(z < chips - 1)
    def _():
        greet(me + 2)

    for unit in range(units):
        kv[me, unit] = own_ref[unit]
    shape = (1, facts.shape[2])
    for slot in range(2):
        for g in range(groups):
            unit = slot * groups + g
            for base, ref in ((0, own_k_scale), (2 * groups, own_v_scale)):
                one = ref[slot : slot + 1, g : g + 1].astype(jnp.float32)
                facts[me, base + unit : base + unit + 1, :] = jnp.broadcast_to(one, shape)
    facts[me, 4 * groups : 4 * groups + 1, :] = jnp.full(
        shape, block_place[0].astype(jnp.float32)
    )

    @pl.when((z > 0) & (z < chips - 1))
    def _():
        pl.semaphore_wait(barrier, 5)

    @pl.when((z == 0) | (z == chips - 1))
    def _():
        pl.semaphore_wait(barrier, 4)

    def move(origin, unit, sems, target):
        return pltpu.make_async_remote_copy(
            src_ref=kv.at[origin, unit], dst_ref=kv.at[origin, unit],
            send_sem=sems.at[origin // 2, unit], recv_sem=recv.at[origin, unit],
            device_id={"ctx": target}, device_id_type=pl.DeviceIdType.MESH,
        )

    def move_facts(origin, sems, target):
        return pltpu.make_async_remote_copy(
            src_ref=facts.at[origin], dst_ref=facts.at[origin],
            send_sem=sems.at[origin // 2, units], recv_sem=recv.at[origin, units],
            device_id={"ctx": target}, device_id_type=pl.DeviceIdType.MESH,
        )

    def send_own(sems, target):
        move_facts(me, sems, target).start()
        for unit in range(units):
            move(me, unit, sems, target).start()

    @pl.when(z < chips - 1)
    def _():
        send_own(send_right, me + 2)

    @pl.when(z > 0)
    def _():
        send_own(send_left, me - 2)

    send_own(send_beside, beside)

    def on(chip, action):
        action(send_beside, beside)

        @pl.when((chip < z) & (z < chips - 1))
        def _():
            action(send_right, me + 2)

        @pl.when((chip > z) & (z > 0))
        def _():
            action(send_left, me - 2)

    def pass_on(chip, unit, with_facts):
        origin = 2 * chip + core
        move(origin, unit, send_beside, beside).wait_recv()
        on(chip, lambda sems, target: move(origin, unit, sems, target).start())

        @pl.when(with_facts)
        def _():
            move_facts(origin, send_beside, beside).wait_recv()
            on(chip, lambda sems, target: move_facts(origin, sems, target).start())

    def arrive(origin, unit):
        move(origin, unit, send_beside, beside).wait_recv()

    def arrive_facts(origin):
        move_facts(origin, send_beside, beside).wait_recv()

    max_ref[...] = jnp.full(max_ref.shape, masked_value, jnp.float32)
    total_ref[...] = jnp.zeros(total_ref.shape, jnp.float32)
    sum_ref[...] = jnp.zeros(sum_ref.shape, jnp.float32)

    for g in range(groups):
        for h in range(per_group):
            columns = slice((g * per_group + h) * head_dim, (g * per_group + h + 1) * head_dim)
            for row in range(2):
                query_ref[row, g, h] = q_ref[row * block_len : (row + 1) * block_len, columns].T

    def gain_row(origin, slot, g):
        low = facts[origin, slot * groups : (slot + 1) * groups, :].astype(jnp.float32)
        row = low[0:1, :]
        for other in range(1, groups):
            row = jnp.where(g == other, low[other : other + 1, :], row)
        return row * rate

    def scale_row(origin, slot, g):
        base = 2 * groups + slot * groups
        low = facts[origin, base : base + groups, :].astype(jnp.float32)
        row = low[0:1, :]
        for other in range(1, groups):
            row = jnp.where(g == other, low[other : other + 1, :], row)
        return row

    def place_row(origin):
        return facts[origin, 4 * groups : 4 * groups + 1, :].astype(jnp.float32)

    def visit(parts, row, g, diagonal=False, blend=None):
        turned = [(key, value.T, gain, scale) for key, value, gain, scale in parts]
        if diagonal:
            shape = (block_len, block_len)
            visible = lax.broadcasted_iota(jnp.int32, shape, 0) <= lax.broadcasted_iota(
                jnp.int32, shape, 1
            )
        if blend is not None:
            is_low, low_share, high_share = blend

        cut = block_len // 2

        def held(ref, index):
            if blend is None:
                return ref[(row, g) + index]
            return jnp.where(is_low[:, :cut], ref[(0, g) + index], ref[(1, g) + index])

        def keep(ref, index, value):
            if blend is None:
                ref[(row, g) + index] = value
            else:
                share = is_low[:, :cut]
                ref[(0, g) + index] = jnp.where(share, value, ref[(0, g) + index])
                ref[(1, g) + index] = jnp.where(share, ref[(1, g) + index], value)

        steps = [(h, slice(n * cut, (n + 1) * cut)) for h in range(per_group) for n in range(block_len // cut)]

        def score(step):
            h, columns = steps[step]
            at = (h, slice(None), columns)
            if blend is None:
                query = query_ref[(row, g) + at]
            else:
                query = (
                    query_ref[(0, g) + at] * low_share[:, :cut]
                    + query_ref[(1, g) + at] * high_share[:, :cut]
                )
            result = [
                jnp.dot(key, query, preferred_element_type=jnp.float32) for key, _, _, _ in turned
            ]
            if diagonal:
                result[-1] = jnp.where(visible[:, columns], result[-1], masked_value)
            return result

        def weigh(step, scores):
            h, columns = steps[step]
            line = (slice(h, h + 1), columns)
            old = held(max_ref, line)
            top = old
            for part, (_, _, gain, _) in zip(scores, turned):
                top = jnp.maximum(top, jnp.max(part, axis=0, keepdims=True) * gain[:, :cut])
            factor = jnp.exp2(old - top)
            total = factor * held(total_ref, line)
            rounded = []
            for part, (_, _, gain, _) in zip(scores, turned):
                weights = jnp.exp2(part * gain[:, :cut] - top)
                total = total + jnp.sum(weights, axis=0, keepdims=True)
                rounded.append(weights.astype(jnp.bfloat16))
            keep(max_ref, line, top)
            keep(total_ref, line, total)
            return rounded, factor

        def gather(step, rounded, factor):
            h, columns = steps[step]
            at = (h, slice(None), columns)
            running = factor * held(sum_ref, at)
            for part, (_, value, _, scale) in zip(rounded, turned):
                running = running + scale[:, :cut] * jnp.dot(
                    value, part, preferred_element_type=jnp.float32
                )
            keep(sum_ref, at, running)

        depth, lag = 2, 1
        scores = {}
        waiting = {}
        for step in range(depth):
            scores[step] = score(step)
        for step in range(len(steps) + lag):
            if step + depth < len(steps):
                scores[step + depth] = score(step + depth)
            if step >= lag:
                gather(step - lag, *waiting.pop(step - lag))
            if step < len(steps):
                waiting[step] = weigh(step, scores.pop(step))

    def part_of(origin, slot, g):
        unit = slot * groups + g
        return (
            kv[origin, unit, :, :head_dim], kv[origin, unit, :, head_dim:],
            gain_row(origin, slot, g), scale_row(origin, slot, g),
        )

    def visit_picked(origin, g):
        is_low = place_row(origin) < place_row(me)
        low_share = is_low.astype(jnp.float32)
        high_share = 1.0 - low_share
        low, high = part_of(origin, 0, g), part_of(origin, 1, g)
        low_bits, high_bits = low_share.astype(jnp.bfloat16), high_share.astype(jnp.bfloat16)
        narrow = (slice(None), slice(0, head_dim))
        part = (
            low[0] * low_bits[narrow] + high[0] * high_bits[narrow],
            low[1] * low_bits[narrow] + high[1] * high_bits[narrow],
            jnp.where(is_low, low[2], high[2]),
            jnp.where(is_low, low[3], high[3]),
        )
        visit([part], None, g, blend=(is_low, low_bits, high_bits))

    def pass_near(unit):
        pass_on(first, unit, unit == 0)

        @pl.when(middle == 1)
        def _():
            pass_on(second, unit, unit == 0)

    @pl.loop(0, groups)
    def _(g):
        visit([part_of(me, 0, g)], 0, g, diagonal=True)

    @pl.loop(0, groups)
    def _(g):
        visit([part_of(me, 1, g)], 1, g, diagonal=True)

    def attend_chip(chip):
        def pair(g):
            visit([part_of(2 * chip, 0, g), part_of(2 * chip + 1, 0, g)], 1, g)

        return pair

    @pl.loop(0, groups)
    def _(g):
        arrive(beside, g)

        @pl.when(g == 0)
        def _():
            arrive_facts(beside)

        attend_chip(z)(g)

    @pl.loop(0, groups)
    def _(g):
        arrive(beside, groups + g)
        visit_picked(beside, g)

    for unit in range(units):
        pass_near(unit)

    @pl.loop(0, chips - 1)
    def _(j):
        chip = first * ((1 - j) * (2 - j) // 2) + second * (j * (2 - j)) + third * (j * (j - 1) // 2)
        step = middle + j - 1
        passing = second + (third - second) * step

        @pl.loop(0, groups)
        def _(g):
            @pl.when((j >= 1) & (step <= 1))
            def _():
                pass_on(passing, g, g == 0)

            arrive(2 * chip + 1 - core, g)

            @pl.when(g == 0)
            def _():
                arrive_facts(2 * chip + 1 - core)

            attend_chip(chip)(g)

        @pl.loop(0, groups)
        def _(g):
            @pl.when((j >= 1) & (step <= 1))
            def _():
                pass_on(passing, groups + g, False)

            visit_picked(2 * chip + core, g)
            arrive(2 * chip + 1 - core, groups + g)
            visit_picked(2 * chip + 1 - core, g)

    @pl.loop(0, 2)
    def _(row):
        rows = pl.ds(pl.multiple_of(row * block_len, block_len), block_len)
        for g in range(groups):
            for h in range(per_group):
                start = (g * per_group + h) * head_dim
                mean = sum_ref[row, g, h] / total_ref[row, g, h : h + 1, :]
                attended[rows, start : start + head_dim] = mean.astype(attended.dtype).T

    def first_copy(c):
        near = along_x + (c % 2) * (along_y - along_x)
        return pltpu.make_async_remote_copy(
            src_ref=terms.at[c, pl.ds(0, 2)], dst_ref=arrived.at[c],
            send_sem=send_one.at[c], recv_sem=recv_one.at[c],
            device_id={"head": near}, device_id_type=pl.DeviceIdType.MESH,
        )

    def second_copy(c):
        far = along_y + (c % 2) * (along_x - along_y)
        return pltpu.make_async_remote_copy(
            src_ref=passed.at[c], dst_ref=ended.at[c],
            send_sem=send_two.at[c], recv_sem=recv_two.at[c],
            device_id={"head": far}, device_id_type=pl.DeviceIdType.MESH,
        )

    @pl.loop(0, chunks + 2 * LAG)
    def _(t):
        @pl.when(t < chunks)
        def _():
            @pl.when(t + 2 < chunks)
            def _():
                fetch(t + 2).start()

            fetch(t).wait()
            term = jnp.dot(
                attended[...], held_w[t % 3], preferred_element_type=jnp.float32
            ).astype(jnp.bfloat16)
            for owner in range(4):
                over_x = (head + owner) % 2
                over_y = (head // 2 + owner // 2) % 2
                place = 3 - over_x - over_y - over_x + (t % 2) * (over_x - over_y)
                terms[t, place] = term[owner * part : (owner + 1) * part]
            first_copy(t).start()

        @pl.when((t >= LAG) & (t < chunks + LAG))
        def _():
            c = t - LAG
            first_copy(c).wait()
            passed[c] = (
                arrived[c, 0].astype(jnp.float32) + terms[c, 2].astype(jnp.float32)
            ).astype(jnp.bfloat16)
            second_copy(c).start()

        @pl.when(t >= 2 * LAG)
        def _():
            c = t - 2 * LAG
            second_copy(c).wait()
            columns = pl.ds(pl.multiple_of(c * step_columns, step_columns), step_columns)
            o_ref[:, columns] = (
                arrived[c, 1].astype(jnp.float32)
                + terms[c, 3].astype(jnp.float32)
                + ended[c].astype(jnp.float32)
            ).astype(jnp.bfloat16)

    def sent(origin, sems, target):
        move_facts(origin, sems, target).wait_send()
        for unit in range(units):
            move(origin, unit, sems, target).wait_send()

    @pl.when(z < chips - 1)
    def _():
        sent(me, send_right, me + 2)

    @pl.when(z > 0)
    def _():
        sent(me, send_left, me - 2)

    sent(me, send_beside, beside)

    @pl.loop(0, chips)
    def _(chip):
        @pl.when(chip != z)
        def _():
            on(chip, lambda sems, target: sent(2 * chip + core, sems, target))


def mix(query, keys, values, k_scale, v_scale, block_place, weight):
    rows, head_count, head_dim = query.shape
    depth, columns = weight.shape
    groups = keys.shape[1]
    slots = block_place.shape[0]
    block_len = rows // slots
    devices = lax.axis_size("ctx")
    chips = devices // 2
    units = slots * groups
    per_group = head_count // groups
    width = 2 * head_dim
    part = rows // lax.axis_size("head")
    step = COLUMN_STEP
    chunks = columns // step
    own = jnp.concatenate([keys, values], axis=2).reshape(slots, block_len, groups, width)
    own = own.transpose(0, 2, 1, 3).reshape(units, block_len, width)
    state = (2, groups, per_group)
    pairs = (2 * devices + 1) * block_len * block_len * head_count
    whole = pl.BlockSpec(memory_space=pltpu.VMEM)
    return pl.pallas_call(
        functools.partial(
            mix_kernel, math.log2(math.e) / math.sqrt(head_dim), per_group, head_dim, chunks
        ),
        in_specs=[pl.BlockSpec(memory_space=pltpu.SMEM)]
        + [whole] * 4
        + [pl.BlockSpec(memory_space=pl.ANY)],
        out_specs=whole,
        scratch_shapes=[
            pltpu.VMEM((devices, units, block_len, width), jnp.bfloat16),
            pltpu.VMEM((devices, 16, width), jnp.float32),
            pltpu.VMEM(state + (head_dim, block_len), jnp.bfloat16),
            pltpu.VMEM(state + (block_len,), jnp.float32),
            pltpu.VMEM(state + (block_len,), jnp.float32),
            pltpu.VMEM(state + (head_dim, block_len), jnp.float32),
            pltpu.VMEM((rows, depth), jnp.bfloat16),
            pltpu.VMEM((3, depth, step), jnp.bfloat16),
            pltpu.VMEM((chunks, 4, part, step), jnp.bfloat16),
            pltpu.VMEM((chunks, 2, part, step), jnp.bfloat16),
            pltpu.VMEM((chunks, part, step), jnp.bfloat16),
            pltpu.VMEM((chunks, part, step), jnp.bfloat16),
            pltpu.SemaphoreType.DMA((devices, units + 1)),
            pltpu.SemaphoreType.DMA((chips, units + 1)),
            pltpu.SemaphoreType.DMA((chips, units + 1)),
            pltpu.SemaphoreType.DMA((chips, units + 1)),
            pltpu.SemaphoreType.DMA((3,)),
            pltpu.SemaphoreType.DMA((chunks,)),
            pltpu.SemaphoreType.DMA((chunks,)),
            pltpu.SemaphoreType.DMA((chunks,)),
            pltpu.SemaphoreType.DMA((chunks,)),
        ],
        out_shape=jax.ShapeDtypeStruct((part, columns), jnp.bfloat16),
        compiler_params=pltpu.CompilerParams(
            collective_id=0, has_side_effects=True, vmem_limit_bytes=47 * 1024 * 1024
        ),
        cost_estimate=pl.CostEstimate(
            flops=4 * pairs * head_dim + 2 * rows * depth * columns,
            bytes_accessed=2 * depth * columns, transcendentals=pairs,
        ),
    )(
        block_place, own, k_scale, v_scale,
        query.reshape(rows, head_count * head_dim), weight,
    )


def body(query, keys, values, k_scale, v_scale, block_place, out_weight):
    rows, head_count, head_dim = query.shape
    group_count = keys.shape[1]
    slots = block_place.shape[0]
    devices = lax.axis_size("ctx")
    blocks = slots * devices
    block_len = rows // slots
    if lax.axis_size("head") == 4 and devices == 8 and slots == 2 and block_len == 2 * head_dim:
        return mix(query, keys, values, k_scale, v_scale, block_place, out_weight)
    width = group_count * head_dim
    facts = jnp.concatenate(
        [k_scale, v_scale, block_place[:, None].astype(jnp.bfloat16)], axis=1
    )
    facts = jnp.pad(facts, ((0, 16 - slots), (0, block_len - facts.shape[1])))

    def payload(slot):
        part = slice(slot * block_len, (slot + 1) * block_len)
        key = keys[part].reshape(block_len, width)
        key = jnp.pad(key, ((0, 0), (0, block_len - width))) if width < block_len else key
        return [key, values[part].reshape(block_len, width).T]

    low_part = lax.all_gather(jnp.concatenate(payload(0) + [facts]), "ctx", axis=0)
    high_part = lax.all_gather(jnp.concatenate(payload(1)), "ctx", axis=0)
    base = block_len + width
    all_facts = low_part[:, base : base + slots, : 2 * group_count + 1].reshape(blocks, -1)
    all_facts = all_facts.astype(jnp.float32)
    places = all_facts[:, -1].astype(jnp.int32)
    ids = jnp.arange(blocks, dtype=jnp.int32)
    order = jnp.sum(jnp.where(places[None, :] == ids[:, None], ids[None, :], 0), axis=1)
    rate = math.log2(math.e) / math.sqrt(head_dim)
    key_gain = (all_facts[:, :group_count] * rate).T.reshape(-1)
    value_gain = all_facts[:, group_count : 2 * group_count].T.reshape(-1)
    known = (order, block_place, key_gain, value_gain)
    flat = query.reshape(rows, head_count * head_dim)
    state = attend(known, flat, low_part, group_count, head_dim, 1)
    low = attend(known, flat, low_part, group_count, head_dim, 0)
    high = attend(known, flat, high_part, group_count, head_dim, 1, state)
    term = jnp.dot(jnp.concatenate([low, high]), out_weight, preferred_element_type=jnp.float32)
    return lax.psum_scatter(
        term.astype(jnp.bfloat16), "head", scatter_dimension=0, tiled=True
    )


def solution(mesh):
    placed = (
        P("ctx", "head", None),
        P("ctx", "head", None),
        P("ctx", "head", None),
        P("ctx", "head"),
        P("ctx", "head"),
        P("ctx"),
        P("head", None),
    )
    return jax.shard_map(
        body, mesh=mesh, in_specs=placed, out_specs=P(("ctx", "head"), None), check_vma=False
    )
```

```python
import functools
import math

import jax
import jax.numpy as jnp
from jax import lax
from jax.experimental import pallas as pl
from jax.experimental.pallas import tpu as pltpu
from jax.sharding import PartitionSpec as P

masked_value = -1e30
COLUMN_STEP = 256
LAG = 6


def attend_kernel(
    per_group, block_len, head_dim, blocks, first_slot, later,
    order, own, key_gain, value_gain,
    q_ref, k_ref, vt_ref, *refs,
):
    group = pl.program_id(0)
    query_ref = refs[-1]
    if later:
        old_max, old_total, old_sum, o_ref, max_ref, total_ref, sum_ref = refs[:-1]
    elif first_slot == 0:
        o_ref, max_ref, total_ref, sum_ref = refs[:-1]
    else:
        max_ref, total_ref, sum_ref = refs[:-1]
    place = own[first_slot]
    for h in range(per_group):
        query_ref[h] = q_ref[:, h * head_dim : (h + 1) * head_dim].T

    def visit(indices, diagonal):
        found = [order[index] for index in indices]
        keys = [k_ref[lax.div(block, 2)] for block in found]
        values = [vt_ref[lax.div(block, 2)] for block in found]
        gains = [key_gain[group * blocks + block] for block in found]
        scales = [value_gain[group * blocks + block] for block in found]
        if diagonal:
            shape = (block_len, block_len)
            visible = lax.broadcasted_iota(jnp.int32, shape, 0) <= lax.broadcasted_iota(
                jnp.int32, shape, 1
            )

        def score(h):
            result = [
                jnp.dot(key, query_ref[h], preferred_element_type=jnp.float32) for key in keys
            ]
            if diagonal:
                result[-1] = jnp.where(visible, result[-1], masked_value)
            return result

        def weigh(h, scores):
            old = max_ref[h : h + 1, :]
            top = old
            for part, gain in zip(scores, gains):
                top = jnp.maximum(top, jnp.max(part, axis=0, keepdims=True) * gain)
            factor = jnp.exp2(old - top)
            total = factor * total_ref[h : h + 1, :]
            rounded = []
            for part, gain in zip(scores, gains):
                weights = jnp.exp2(part * gain - top)
                total = total + jnp.sum(weights, axis=0, keepdims=True)
                rounded.append(weights.astype(jnp.bfloat16))
            max_ref[h : h + 1, :] = top
            total_ref[h : h + 1, :] = total
            return rounded, factor

        def gather(h, rounded, factor):
            running = factor * sum_ref[h]
            for part, value, scale in zip(rounded, values, scales):
                running = running + scale * jnp.dot(
                    value, part, preferred_element_type=jnp.float32
                )
            sum_ref[h] = running

        scores = score(0)
        waiting = None
        for h in range(per_group):
            upcoming = score(h + 1) if h + 1 < per_group else None
            if waiting is not None:
                gather(h - 1, *waiting)
            waiting = weigh(h, scores)
            scores = upcoming
        gather(per_group - 1, *waiting)

    half = blocks // 2
    if later:
        max_ref[...] = old_max[...]
        total_ref[...] = old_total[...]
        sum_ref[...] = old_sum[...]
        start, stop = half, place
    else:
        max_ref[...] = jnp.full(max_ref.shape, masked_value, jnp.float32)
        total_ref[...] = jnp.zeros(total_ref.shape, jnp.float32)
        sum_ref[...] = jnp.zeros(sum_ref.shape, jnp.float32)
        start, stop = 0, (place if first_slot == 0 else half)
    pairs = (stop - start) // 2

    @pl.loop(0, pairs)
    def _(pair):
        visit([start + 2 * pair, start + 2 * pair + 1], False)

    if later or first_slot == 0:
        odd = (stop - start) - 2 * pairs

        @pl.when(odd == 1)
        def _():
            visit([place - 1, place], True)

        @pl.when(odd == 0)
        def _():
            visit([place], True)

        for h in range(per_group):
            columns = slice(h * head_dim, (h + 1) * head_dim)
            mean = sum_ref[h] / total_ref[h : h + 1, :]
            o_ref[:, columns] = mean.T.astype(o_ref.dtype)
    elif half % 2:
        visit([half - 1], False)


def attend(facts, query, gathered, group_count, head_dim, slot, state=None):
    rows, width = query.shape
    devices = gathered.shape[0]
    block_len = rows // 2
    group_width = width // group_count
    per_group = group_width // head_dim
    heads = group_count * per_group
    blocks = facts[0].shape[0]
    later = state is not None
    tiles = blocks // 4 if later or slot == 0 else blocks // 2
    pairs = tiles * block_len * block_len * heads
    row_spec = pl.BlockSpec((per_group, block_len), lambda g, *_: (g, 0))
    sum_spec = pl.BlockSpec((per_group, head_dim, block_len), lambda g, *_: (g, 0, 0))
    state_specs = [row_spec, row_spec, sum_spec]
    row_shape = (per_group, block_len)
    sum_shape = (per_group, head_dim, block_len)
    first_value = block_len // head_dim
    outs = ([pl.BlockSpec((block_len, group_width), lambda g, *_: (0, g))],
            [jax.ShapeDtypeStruct((block_len, width), jnp.bfloat16)])
    scratch = [
        pltpu.VMEM(row_shape, jnp.float32),
        pltpu.VMEM(row_shape, jnp.float32),
        pltpu.VMEM(sum_shape, jnp.float32),
    ]
    if not later and slot == 1:
        outs = (state_specs, [
            jax.ShapeDtypeStruct((heads, block_len), jnp.float32),
            jax.ShapeDtypeStruct((heads, block_len), jnp.float32),
            jax.ShapeDtypeStruct((heads, head_dim, block_len), jnp.float32),
        ])
        scratch = []
    scratch.append(pltpu.VMEM((per_group, head_dim, block_len), jnp.bfloat16))
    results = pl.pallas_call(
        functools.partial(
            attend_kernel, per_group, block_len, head_dim, blocks, slot, later
        ),
        grid_spec=pltpu.PrefetchScalarGridSpec(
            num_scalar_prefetch=4,
            grid=(group_count,),
            in_specs=[
                pl.BlockSpec((block_len, group_width), lambda g, *_: (slot, g)),
                pl.BlockSpec((devices, block_len, head_dim), lambda g, *_: (0, 0, g)),
                pl.BlockSpec(
                    (devices, head_dim, block_len), lambda g, *_: (0, first_value + g, 0)
                ),
            ] + (state_specs if later else []),
            out_specs=outs[0],
            scratch_shapes=scratch,
        ),
        out_shape=outs[1],
        compiler_params=pltpu.CompilerParams(vmem_limit_bytes=40 * 1024 * 1024),
        cost_estimate=pl.CostEstimate(
            flops=4 * pairs * head_dim, bytes_accessed=4 << 20, transcendentals=pairs
        ),
    )(*facts, query, gathered, gathered, *(state if later else ()))
    return results if len(results) > 1 else results[0]


def mix_kernel(
    rate, per_group, head_dim, chunks,
    block_place, own_ref, own_k_scale, own_v_scale, q_ref, w_ref, o_ref,
    kv, facts, query_ref, max_ref, total_ref, sum_ref,
    attended, held_w, terms, arrived, passed, ended,
    recv, send_right, send_left, send_beside,
    load_w, send_one, recv_one, send_two, recv_two,
):
    groups = kv.shape[1] // 2
    units = kv.shape[1]
    block_len = kv.shape[2]
    chips = kv.shape[0] // 2
    me = lax.axis_index("ctx")
    z, core = me // 2, me % 2
    beside = 2 * z + 1 - core
    half = z // 2
    middle = (z % 2 + half) % 2
    first = z + 1 - 2 * (z % 2)
    second = 2 - half
    third = 3 * (1 - half)

    head = lax.axis_index("head")
    along_x = head + 1 - 2 * (head % 2)
    along_y = (head + 2) % 4
    step_columns = held_w.shape[2]
    part = o_ref.shape[0]

    def fetch(chunk):
        columns = pl.ds(pl.multiple_of(chunk * step_columns, step_columns), step_columns)
        return pltpu.make_async_copy(
            w_ref.at[:, columns], held_w.at[chunk % 3], load_w.at[chunk % 3]
        )

    fetch(0).start()
    fetch(1).start()

    barrier = pltpu.get_barrier_semaphore()

    def greet(device):
        pl.semaphore_signal(
            barrier, inc=1, device_id={"ctx": device}, device_id_type=pl.DeviceIdType.MESH
        )

    for partner in (along_x, along_y):
        pl.semaphore_signal(
            barrier, inc=1, device_id={"head": partner}, device_id_type=pl.DeviceIdType.MESH
        )
    greet(beside)

    @pl.when(z > 0)
    def _():
        greet(me - 2)

    @pl.when(z < chips - 1)
    def _():
        greet(me + 2)

    for unit in range(units):
        kv[me, unit] = own_ref[unit]
    shape = (1, facts.shape[2])
    listed = [
        jnp.broadcast_to(ref[slot : slot + 1, g : g + 1].astype(jnp.float32), shape)
        for ref in (own_k_scale, own_v_scale)
        for slot in range(2)
        for g in range(groups)
    ]
    listed.append(jnp.full(shape, block_place[0].astype(jnp.float32)))
    spare = facts.shape[1] - len(listed)
    listed.append(jnp.zeros((spare,) + shape[1:], jnp.float32))
    facts[me] = jnp.concatenate(listed, axis=0).astype(facts.dtype)

    @pl.when((z > 0) & (z < chips - 1))
    def _():
        pl.semaphore_wait(barrier, 5)

    @pl.when((z == 0) | (z == chips - 1))
    def _():
        pl.semaphore_wait(barrier, 4)

    def move(origin, unit, sems, target):
        return pltpu.make_async_remote_copy(
            src_ref=kv.at[origin, unit], dst_ref=kv.at[origin, unit],
            send_sem=sems.at[origin // 2, unit], recv_sem=recv.at[origin, unit],
            device_id={"ctx": target}, device_id_type=pl.DeviceIdType.MESH,
        )

    def move_facts(origin, sems, target):
        return pltpu.make_async_remote_copy(
            src_ref=facts.at[origin], dst_ref=facts.at[origin],
            send_sem=sems.at[origin // 2, units], recv_sem=recv.at[origin, units],
            device_id={"ctx": target}, device_id_type=pl.DeviceIdType.MESH,
        )

    def send_own(slot):
        def start(sems, target):
            if slot == 0:
                move_facts(me, sems, target).start()
            for unit in range(slot * groups, (slot + 1) * groups):
                move(me, unit, sems, target).start()

        @pl.when(z < chips - 1)
        def _():
            start(send_right, me + 2)

        @pl.when(z > 0)
        def _():
            start(send_left, me - 2)

        start(send_beside, beside)

    send_own(0)

    def on(chip, action):
        action(send_beside, beside)

        @pl.when((chip < z) & (z < chips - 1))
        def _():
            action(send_right, me + 2)

        @pl.when((chip > z) & (z > 0))
        def _():
            action(send_left, me - 2)

    def pass_on(chip, unit, with_facts):
        origin = 2 * chip + core
        move(origin, unit, send_beside, beside).wait_recv()
        on(chip, lambda sems, target: move(origin, unit, sems, target).start())

        @pl.when(with_facts)
        def _():
            move_facts(origin, send_beside, beside).wait_recv()
            on(chip, lambda sems, target: move_facts(origin, sems, target).start())

    def arrive(origin, unit):
        move(origin, unit, send_beside, beside).wait_recv()

    def arrive_facts(origin):
        move_facts(origin, send_beside, beside).wait_recv()

    max_ref[...] = jnp.full(max_ref.shape, masked_value, jnp.float32)
    total_ref[...] = jnp.zeros(total_ref.shape, jnp.float32)
    sum_ref[...] = jnp.zeros(sum_ref.shape, jnp.float32)

    for g in range(groups):
        for h in range(per_group):
            columns = slice((g * per_group + h) * head_dim, (g * per_group + h + 1) * head_dim)
            for row in range(2):
                query_ref[row, g, h] = q_ref[row * block_len : (row + 1) * block_len, columns].T

    def gain_row(origin, slot, g):
        low = facts[origin, slot * groups : (slot + 1) * groups, :].astype(jnp.float32)
        row = low[0:1, :]
        for other in range(1, groups):
            row = jnp.where(g == other, low[other : other + 1, :], row)
        return row * rate

    def scale_row(origin, slot, g):
        base = 2 * groups + slot * groups
        low = facts[origin, base : base + groups, :].astype(jnp.float32)
        row = low[0:1, :]
        for other in range(1, groups):
            row = jnp.where(g == other, low[other : other + 1, :], row)
        return row

    def place_row(origin):
        return facts[origin, 4 * groups : 4 * groups + 1, :].astype(jnp.float32)

    def visit(parts, row, g, diagonal=False, blend=None):
        turned = [(key, value.T, gain, scale) for key, value, gain, scale in parts]
        if diagonal:
            shape = (block_len, block_len)
            visible = lax.broadcasted_iota(jnp.int32, shape, 0) <= lax.broadcasted_iota(
                jnp.int32, shape, 1
            )
        if blend is not None:
            is_low, low_share, high_share = blend

        cut = facts.shape[2]

        def held(ref, index):
            if blend is None:
                return ref[(row, g) + index]
            return jnp.where(is_low, ref[(0, g) + index], ref[(1, g) + index])

        def keep(ref, index, value):
            if blend is None:
                ref[(row, g) + index] = value
            else:
                share = is_low
                ref[(0, g) + index] = jnp.where(share, value, ref[(0, g) + index])
                ref[(1, g) + index] = jnp.where(share, ref[(1, g) + index], value)

        steps = [(h, slice(n * cut, (n + 1) * cut)) for h in range(per_group) for n in range(block_len // cut)]

        def score(step):
            h, columns = steps[step]
            at = (h, slice(None), columns)
            if blend is None:
                query = query_ref[(row, g) + at]
            else:
                query = (
                    query_ref[(0, g) + at] * low_share
                    + query_ref[(1, g) + at] * high_share
                )
            result = [
                jnp.dot(key, query, preferred_element_type=jnp.float32) for key, _, _, _ in turned
            ]
            if diagonal:
                result[-1] = jnp.where(visible[:, columns], result[-1], masked_value)
            return result

        def weigh(step, scores):
            h, columns = steps[step]
            line = (slice(h, h + 1), columns)
            old = held(max_ref, line)
            top = old
            for part, (_, _, gain, _) in zip(scores, turned):
                top = jnp.maximum(top, jnp.max(part, axis=0, keepdims=True) * gain)
            factor = jnp.exp2(old - top)
            total = factor * held(total_ref, line)
            rounded = []
            for part, (_, _, gain, _) in zip(scores, turned):
                weights = jnp.exp2(part * gain - top)
                total = total + jnp.sum(weights, axis=0, keepdims=True)
                rounded.append(weights.astype(jnp.bfloat16))
            keep(max_ref, line, top)
            keep(total_ref, line, total)
            return rounded, factor

        def gather(step, rounded, factor):
            h, columns = steps[step]
            at = (h, slice(None), columns)
            running = factor * held(sum_ref, at)
            for part, (_, value, _, scale) in zip(rounded, turned):
                running = running + scale * jnp.dot(
                    value, part, preferred_element_type=jnp.float32
                )
            keep(sum_ref, at, running)

        depth, lag = 2, 1
        scores = {}
        waiting = {}
        for step in range(depth):
            scores[step] = score(step)
        for step in range(len(steps) + lag):
            if step + depth < len(steps):
                scores[step + depth] = score(step + depth)
            if step >= lag:
                gather(step - lag, *waiting.pop(step - lag))
            if step < len(steps):
                waiting[step] = weigh(step, scores.pop(step))

    def part_of(origin, slot, g):
        unit = slot * groups + g
        return (
            kv[origin, unit, :, :head_dim], kv[origin, unit, :, head_dim:],
            gain_row(origin, slot, g), scale_row(origin, slot, g),
        )

    def visit_picked(origin, g):
        is_low = place_row(origin) < place_row(me)
        low_share = is_low.astype(jnp.float32)
        high_share = 1.0 - low_share
        low, high = part_of(origin, 0, g), part_of(origin, 1, g)
        low_bits, high_bits = low_share.astype(jnp.bfloat16), high_share.astype(jnp.bfloat16)
        part = (
            low[0] * low_bits + high[0] * high_bits,
            low[1] * low_bits + high[1] * high_bits,
            jnp.where(is_low, low[2], high[2]),
            jnp.where(is_low, low[3], high[3]),
        )
        visit([part], None, g, blend=(is_low, low_bits, high_bits))

    def pass_near(unit):
        pass_on(first, unit, unit == 0)

        @pl.when(middle == 1)
        def _():
            pass_on(second, unit, unit == 0)

    @pl.loop(0, groups)
    def _(g):
        visit([part_of(me, 0, g)], 0, g, diagonal=True)

    send_own(1)

    @pl.loop(0, groups)
    def _(g):
        visit([part_of(me, 1, g)], 1, g, diagonal=True)

    for unit in range(groups):
        pass_near(unit)

    def attend_chip(chip):
        def pair(g):
            visit([part_of(2 * chip, 0, g), part_of(2 * chip + 1, 0, g)], 1, g)

        return pair

    @pl.loop(0, groups)
    def _(g):
        arrive(beside, g)

        @pl.when(g == 0)
        def _():
            arrive_facts(beside)

        attend_chip(z)(g)

    @pl.loop(0, groups)
    def _(g):
        arrive(beside, groups + g)
        visit_picked(beside, g)

    for unit in range(groups, units):
        pass_near(unit)

    farther = second + (third - second) * middle

    def pass_both(chip, slot):
        for unit in range(slot * groups, (slot + 1) * groups):
            pass_on(chip, unit, unit == 0)

    @pl.loop(0, chips - 1)
    def _(j):
        chip = first * ((1 - j) * (2 - j) // 2) + second * (j * (2 - j)) + third * (j * (j - 1) // 2)
        other = 2 * chip + 1 - core
        arrive_facts(other)

        @pl.loop(0, groups)
        def _(g):
            arrive(other, g)
            attend_chip(chip)(g)

            @pl.when((j == 1) & (g == 0))
            def _():
                pass_both(farther, 1)

        @pl.when(j == 0)
        def _():
            pass_both(farther, 0)

        @pl.loop(0, groups)
        def _(g):
            @pl.when((j == 2) & (middle == 0))
            def _():
                pass_on(third, groups + g, False)

            visit_picked(2 * chip + core, g)

            @pl.when((j == 1) & (g == groups - 1) & (middle == 0))
            def _():
                pass_both(third, 0)

            arrive(other, groups + g)
            visit_picked(other, g)

            @pl.when(j == chips - 2)
            def _():
                for row in range(2):
                    for h in range(per_group):
                        start = pl.multiple_of((g * per_group + h) * head_dim, head_dim)
                        mean = sum_ref[row, g, h] / total_ref[row, g, h : h + 1, :]
                        attended[
                            row * block_len : (row + 1) * block_len, pl.ds(start, head_dim)
                        ] = mean.astype(attended.dtype).T

    def first_copy(c):
        near = along_x + (c % 2) * (along_y - along_x)
        return pltpu.make_async_remote_copy(
            src_ref=terms.at[c, pl.ds(0, 2)], dst_ref=arrived.at[c],
            send_sem=send_one.at[c], recv_sem=recv_one.at[c],
            device_id={"head": near}, device_id_type=pl.DeviceIdType.MESH,
        )

    def second_copy(c):
        far = along_y + (c % 2) * (along_x - along_y)
        return pltpu.make_async_remote_copy(
            src_ref=passed.at[c], dst_ref=ended.at[c],
            send_sem=send_two.at[c], recv_sem=recv_two.at[c],
            device_id={"head": far}, device_id_type=pl.DeviceIdType.MESH,
        )

    @pl.loop(0, chunks + 2 * LAG)
    def _(t):
        @pl.when(t < chunks)
        def _():
            @pl.when(t + 2 < chunks)
            def _():
                fetch(t + 2).start()

            fetch(t).wait()
            term = jnp.dot(
                attended[...], held_w[t % 3], preferred_element_type=jnp.float32
            ).astype(jnp.bfloat16)
            for owner in range(4):
                over_x = (head + owner) % 2
                over_y = (head // 2 + owner // 2) % 2
                place = 3 - over_x - over_y - over_x + (t % 2) * (over_x - over_y)
                terms[t, place] = term[owner * part : (owner + 1) * part]
            first_copy(t).start()

        @pl.when((t >= LAG) & (t < chunks + LAG))
        def _():
            c = t - LAG
            first_copy(c).wait()
            passed[c] = (
                arrived[c, 0].astype(jnp.float32) + terms[c, 2].astype(jnp.float32)
            ).astype(jnp.bfloat16)
            second_copy(c).start()

        @pl.when(t >= 2 * LAG)
        def _():
            c = t - 2 * LAG
            second_copy(c).wait()
            columns = pl.ds(pl.multiple_of(c * step_columns, step_columns), step_columns)
            o_ref[:, columns] = (
                arrived[c, 1].astype(jnp.float32)
                + terms[c, 3].astype(jnp.float32)
                + ended[c].astype(jnp.float32)
            ).astype(jnp.bfloat16)

    def sent(origin, sems, target):
        move_facts(origin, sems, target).wait_send()
        for unit in range(units):
            move(origin, unit, sems, target).wait_send()

    @pl.when(z < chips - 1)
    def _():
        sent(me, send_right, me + 2)

    @pl.when(z > 0)
    def _():
        sent(me, send_left, me - 2)

    sent(me, send_beside, beside)

    @pl.loop(0, chips)
    def _(chip):
        @pl.when(chip != z)
        def _():
            on(chip, lambda sems, target: sent(2 * chip + core, sems, target))


def mix(query, keys, values, k_scale, v_scale, block_place, weight):
    rows, head_count, head_dim = query.shape
    depth, columns = weight.shape
    groups = keys.shape[1]
    slots = block_place.shape[0]
    block_len = rows // slots
    devices = lax.axis_size("ctx")
    chips = devices // 2
    units = slots * groups
    per_group = head_count // groups
    width = 2 * head_dim
    part = rows // lax.axis_size("head")
    step = COLUMN_STEP
    chunks = columns // step
    own = jnp.concatenate([keys, values], axis=2).reshape(slots, block_len, groups, width)
    own = own.transpose(0, 2, 1, 3).reshape(units, block_len, width)
    state = (2, groups, per_group)
    pairs = (2 * devices + 1) * block_len * block_len * head_count
    whole = pl.BlockSpec(memory_space=pltpu.VMEM)
    return pl.pallas_call(
        functools.partial(
            mix_kernel, math.log2(math.e) / math.sqrt(head_dim), per_group, head_dim, chunks
        ),
        in_specs=[pl.BlockSpec(memory_space=pltpu.SMEM)]
        + [whole] * 4
        + [pl.BlockSpec(memory_space=pl.ANY)],
        out_specs=whole,
        scratch_shapes=[
            pltpu.VMEM((devices, units, block_len, width), jnp.bfloat16),
            pltpu.VMEM((devices, 16, head_dim), jnp.bfloat16),
            pltpu.VMEM(state + (head_dim, block_len), jnp.bfloat16),
            pltpu.VMEM(state + (block_len,), jnp.float32),
            pltpu.VMEM(state + (block_len,), jnp.float32),
            pltpu.VMEM(state + (head_dim, block_len), jnp.float32),
            pltpu.VMEM((rows, depth), jnp.bfloat16),
            pltpu.VMEM((3, depth, step), jnp.bfloat16),
            pltpu.VMEM((chunks, 4, part, step), jnp.bfloat16),
            pltpu.VMEM((chunks, 2, part, step), jnp.bfloat16),
            pltpu.VMEM((chunks, part, step), jnp.bfloat16),
            pltpu.VMEM((chunks, part, step), jnp.bfloat16),
            pltpu.SemaphoreType.DMA((devices, units + 1)),
            pltpu.SemaphoreType.DMA((chips, units + 1)),
            pltpu.SemaphoreType.DMA((chips, units + 1)),
            pltpu.SemaphoreType.DMA((chips, units + 1)),
            pltpu.SemaphoreType.DMA((3,)),
            pltpu.SemaphoreType.DMA((chunks,)),
            pltpu.SemaphoreType.DMA((chunks,)),
            pltpu.SemaphoreType.DMA((chunks,)),
            pltpu.SemaphoreType.DMA((chunks,)),
        ],
        out_shape=jax.ShapeDtypeStruct((part, columns), jnp.bfloat16),
        compiler_params=pltpu.CompilerParams(
            collective_id=0, has_side_effects=True, vmem_limit_bytes=47 * 1024 * 1024
        ),
        cost_estimate=pl.CostEstimate(
            flops=4 * pairs * head_dim + 2 * rows * depth * columns,
            bytes_accessed=2 * depth * columns, transcendentals=pairs,
        ),
    )(
        block_place, own, k_scale, v_scale,
        query.reshape(rows, head_count * head_dim), weight,
    )


def body(query, keys, values, k_scale, v_scale, block_place, out_weight):
    rows, head_count, head_dim = query.shape
    group_count = keys.shape[1]
    slots = block_place.shape[0]
    devices = lax.axis_size("ctx")
    blocks = slots * devices
    block_len = rows // slots
    if lax.axis_size("head") == 4 and devices == 8 and slots == 2 and block_len == 2 * head_dim:
        return mix(query, keys, values, k_scale, v_scale, block_place, out_weight)
    width = group_count * head_dim
    facts = jnp.concatenate(
        [k_scale, v_scale, block_place[:, None].astype(jnp.bfloat16)], axis=1
    )
    facts = jnp.pad(facts, ((0, 16 - slots), (0, block_len - facts.shape[1])))

    def payload(slot):
        part = slice(slot * block_len, (slot + 1) * block_len)
        key = keys[part].reshape(block_len, width)
        key = jnp.pad(key, ((0, 0), (0, block_len - width))) if width < block_len else key
        return [key, values[part].reshape(block_len, width).T]

    low_part = lax.all_gather(jnp.concatenate(payload(0) + [facts]), "ctx", axis=0)
    high_part = lax.all_gather(jnp.concatenate(payload(1)), "ctx", axis=0)
    base = block_len + width
    all_facts = low_part[:, base : base + slots, : 2 * group_count + 1].reshape(blocks, -1)
    all_facts = all_facts.astype(jnp.float32)
    places = all_facts[:, -1].astype(jnp.int32)
    ids = jnp.arange(blocks, dtype=jnp.int32)
    order = jnp.sum(jnp.where(places[None, :] == ids[:, None], ids[None, :], 0), axis=1)
    rate = math.log2(math.e) / math.sqrt(head_dim)
    key_gain = (all_facts[:, :group_count] * rate).T.reshape(-1)
    value_gain = all_facts[:, group_count : 2 * group_count].T.reshape(-1)
    known = (order, block_place, key_gain, value_gain)
    flat = query.reshape(rows, head_count * head_dim)
    state = attend(known, flat, low_part, group_count, head_dim, 1)
    low = attend(known, flat, low_part, group_count, head_dim, 0)
    high = attend(known, flat, high_part, group_count, head_dim, 1, state)
    term = jnp.dot(jnp.concatenate([low, high]), out_weight, preferred_element_type=jnp.float32)
    return lax.psum_scatter(
        term.astype(jnp.bfloat16), "head", scatter_dimension=0, tiled=True
    )


def solution(mesh):
    placed = (
        P("ctx", "head", None),
        P("ctx", "head", None),
        P("ctx", "head", None),
        P("ctx", "head"),
        P("ctx", "head"),
        P("ctx"),
        P("head", None),
    )
    return jax.shard_map(
        body, mesh=mesh, in_specs=placed, out_specs=P(("ctx", "head"), None), check_vma=False
    )
```
